128 devices in a mesh: gx: 8 (over z, core), gy: 16 (over x, y).
Axes of the slice: x: 4, y: 4, z: 4, core: 2. Of those that a mesh axis runs over, the one named last changes fastest.
Arguments:
- tokens: bfloat16 [4096, 4096], P(('gx', 'gy')), may hold values from -3 to 3
- attn_gain: bfloat16 [4096], replicated, may hold values from 0.099609375 to 1.8984375
- mlp_gain: bfloat16 [4096], replicated, may hold values from 0.099609375 to 1.8984375
- w_query: bfloat16 [4096, 4096], P('gx', 'gy'), may hold values from -1 to 1
- w_key: bfloat16 [4096, 1024], P('gx', 'gy'), may hold values from -1 to 1
- value_projection: bfloat16 [4096, 1024], P('gx', 'gy'), may hold values from -0.09375 to 0.09375
- w_out: bfloat16 [4096, 4096], P('gy', 'gx'), may hold values from -0.09375 to 0.09375
- w_gate: bfloat16 [4096, 14336], P('gx', 'gy'), may hold values from -0.09375 to 0.09375
- w_up: bfloat16 [4096, 14336], P('gx', 'gy'), may hold values from -0.09375 to 0.09375
- w_down: bfloat16 [14336, 4096], P('gy', 'gx'), may hold values from -0.046875 to 0.046875
- lengths: int32 [6], replicated, may hold values from 1 to 3072, 4096 in all
- page_table: int32 [128, 2], replicated, may hold values from 0 to 15, as said below
Outputs:
- layer_out: bfloat16 [4096, 4096], P(('gx', 'gy'))
- paged_key_value_cache: bfloat16 [128, 2, 32, 1024], P('gx', None, None, 'gy')
The draws below stay inside these ranges and needn't reach their ends.
Inputs may be any that keep to these rules, and one draw needn't show every extreme that they name: `page_table`: page p belongs to token group p // 16, the tokens of one index of gx. Its owner is an index of gx and its slot is below 16; every pair of owner and slot is taken by exactly one page. Of one token group's pages, 8 owners receive exactly 2 each and the other owners none.
All inputs are finite; a program needn't handle non-finite values.
Results may differ from the reference program's by a relative error of at most 0.025.
The reference program's roundings to bfloat16 on the way (of `normed`, `attended`, `residual`, `normed_mlp` and `hidden`) count: a program that leaves them out, or rounds other values in their place, can miss the bound.
Values may be sent and summed in bfloat16 or wider, within the bound.
A program may use at most 128 MiB of HBM per device.

```python
import math
import jax
import jax.numpy as jnp
import numpy as np
from jax import lax

MODEL_WIDTH = 4096
QUERY_HEAD_COUNT = 32
KEY_VALUE_HEADS = 8
HEAD_WIDTH = 128
FF = 14336
WIN = 4096
PAGE_TOKENS = 32
SEQS = 6
PACK_TOKENS = 4096
PACK_PAGES = 128
CACHE_GROUP_CELLS = 16
CAP = 2
N_GX = 8


def draw_w_query(key, part):
    local_key = jax.random.fold_in(key, 1)
    return (jnp.clip(jax.random.normal(local_key, (MODEL_WIDTH, QUERY_HEAD_COUNT * HEAD_WIDTH), jnp.float32), -6.0, 6.0) * MODEL_WIDTH ** (-0.5)).astype(jnp.bfloat16)


def draw_w_key(key, part):
    local_key = jax.random.fold_in(key, 2)
    return (jnp.clip(jax.random.normal(local_key, (MODEL_WIDTH, KEY_VALUE_HEADS * HEAD_WIDTH), jnp.float32), -6.0, 6.0) * MODEL_WIDTH ** (-0.5)).astype(jnp.bfloat16)


def draw_page_table(key, part):
    groups = PACK_PAGES // CACHE_GROUP_CELLS
    key_order, key_owner, key_slot = jax.random.split(key, 3)
    order = jax.vmap(lambda item: jax.random.permutation(item, CACHE_GROUP_CELLS))(jax.random.split(key_order, groups))
    owners = jax.random.permutation(key_owner, groups)
    slots = jax.vmap(lambda item: jax.random.permutation(item, CACHE_GROUP_CELLS))(jax.random.split(key_slot, groups))
    group_index = jnp.arange(groups, dtype=jnp.int32)[:, None]
    base = (group_index + order // CAP) % groups
    owner = owners[base]
    slot = slots[base, order]
    return jnp.stack([owner.reshape(-1), slot.reshape(-1)], axis=-1).astype(jnp.int32)


def level_of(stream_key, extent, cuts, smallest, largest):
    level, own = 1.0, jax.random.fold_in(stream_key, 6)
    for axis_at, blocks in cuts:
        draws = jnp.exp(jax.random.uniform(jax.random.fold_in(own, axis_at), (blocks,), jnp.float32, smallest / len(cuts), largest / len(cuts)))
        level = level * jnp.repeat(draws, extent[axis_at] // blocks).reshape([-1 if axis == axis_at else 1 for axis in range(len(extent))])
    return level


def profile(number_of, total, bound, lean):
    portions = [(1 << 20) // math.isqrt(standing ** lean) + 1 for standing in range(2, number_of + 1)]
    rest, holding = total - bound - (number_of - 1), [1] * (number_of - 1)
    while rest > 0:
        movable = [i for i in range(number_of - 1) if holding[i] < bound]
        pool, budget = sum([portions[i] for i in movable]), rest
        for i in movable:
            addition = min(bound - holding[i], max(1, budget * portions[i] // pool), rest)
            holding[i] = holding[i] + addition
            rest = rest - addition
    return np.array([bound] + holding)


def uneven_parts(stream_key, amount, total, bound, slope):
    if amount == 2:
        one = jax.random.randint(stream_key, (), max(1, total - bound), min(bound, total - 1) + 1)
        return jnp.stack([one, total - one])
    sizes = jnp.asarray(profile(amount, total, bound, slope), jnp.int32)
    twos = (amount - 1) // 2
    donor, sink = sizes[1:1 + 2 * twos:2], sizes[2:2 + 2 * twos:2]
    margin = jnp.minimum(donor - 1, bound - sink)
    passed = jax.random.randint(jax.random.fold_in(stream_key, 1), (twos,), 0, 1 << 20) % (margin + 1)
    sizes = sizes.at[1:1 + 2 * twos:2].set(donor - passed).at[2:2 + 2 * twos:2].set(sink + passed)
    return sizes[jax.random.permutation(jax.random.fold_in(stream_key, 2), amount)]


def normal_values(stream_key, shape, scale, limit, pieces=(), kind=jnp.bfloat16):
    entries = jax.random.normal(stream_key, shape, jnp.float32) * scale
    if len(pieces) > 0:
        entries = level_of(stream_key, shape, pieces, -0.22, 0.18) * entries
    return jnp.clip(entries, min=-limit, max=limit).astype(kind)


def setup_inputs(seed: int = 0) -> dict:
    arg_keys = jax.random.split(jax.random.key(seed), 13)
    tokens = normal_values(arg_keys[0], (PACK_TOKENS, MODEL_WIDTH), 0.5, 3.0, ((0, 128),))
    attn_gain = jnp.clip(1.0 + 0.18 * jax.random.normal(arg_keys[1], (MODEL_WIDTH,), jnp.float32), 0.099609375, 1.8984375).astype(jnp.bfloat16)
    mlp_gain = jnp.clip(1.0 + 0.18 * jax.random.normal(arg_keys[2], (MODEL_WIDTH,), jnp.float32), 0.099609375, 1.8984375).astype(jnp.bfloat16)
    w_query = draw_w_query(jax.random.fold_in(arg_keys[12], 71), 0)
    w_key = draw_w_key(jax.random.fold_in(arg_keys[12], 71), 0)
    value_projection = normal_values(arg_keys[5], (MODEL_WIDTH, KEY_VALUE_HEADS * HEAD_WIDTH), MODEL_WIDTH ** -0.5, 0.09375, ((0, 8), (1, 16)))
    w_out = normal_values(arg_keys[6], (QUERY_HEAD_COUNT * HEAD_WIDTH, MODEL_WIDTH), (QUERY_HEAD_COUNT * HEAD_WIDTH) ** -0.5, 0.09375, ((0, 16), (1, 8)))
    w_gate = normal_values(arg_keys[7], (MODEL_WIDTH, FF), MODEL_WIDTH ** -0.5, 0.09375, ((0, 8), (1, 16)))
    w_up = normal_values(arg_keys[8], (MODEL_WIDTH, FF), MODEL_WIDTH ** -0.5, 0.09375, ((0, 8), (1, 16)))
    w_down = normal_values(arg_keys[9], (FF, MODEL_WIDTH), FF ** -0.5, 0.046875, ((0, 16), (1, 8)))
    lengths = uneven_parts(arg_keys[10], SEQS, PACK_TOKENS, PACK_TOKENS * 3 // 4, 2).astype(jnp.int32)
    page_table = draw_page_table(jax.random.fold_in(arg_keys[12], 71), 0)
    return dict(tokens=tokens, attn_gain=attn_gain, mlp_gain=mlp_gain, w_query=w_query, w_key=w_key, value_projection=value_projection, w_out=w_out, w_gate=w_gate, w_up=w_up, w_down=w_down, lengths=lengths, page_table=page_table)


rope_base = 10000.0
norm_eps = 1e-05
masked_score = -1e+30

def rms_scale(values, gain):
    floats = values.astype(jnp.float32)
    mean_square = lax.optimization_barrier(jnp.mean(floats * floats, axis=-1, keepdims=True))
    return floats * lax.rsqrt(mean_square + norm_eps) * gain.astype(jnp.float32)

def segment_info(lengths, token_index):
    ends = jnp.cumsum(lengths, dtype=jnp.int32)
    starts = ends - lengths
    inside = (token_index[:, None] >= starts[None, :]).astype(jnp.int32)
    segment = lax.optimization_barrier(jnp.sum(inside, axis=1, dtype=jnp.int32)) - 1
    chosen = (segment[:, None] == jnp.arange(lengths.shape[0], dtype=jnp.int32)[None, :]).astype(jnp.int32)
    token_positions = token_index - lax.optimization_barrier(jnp.sum(chosen * starts[None, :], axis=1, dtype=jnp.int32))
    return (segment, token_positions)

def apply_rotary(values, token_positions):
    half = values.shape[-1] // 2
    freq = rope_base ** (-jnp.arange(half, dtype=jnp.float32) * 2.0 / values.shape[-1])
    angle = token_positions.astype(jnp.float32)[:, None] * freq[None, :]
    cosine = jnp.cos(angle)[:, None, :]
    sine = jnp.sin(angle)[:, None, :]
    first = values[..., :half]
    second = values[..., half:]
    return jnp.concatenate([first * cosine - second * sine, second * cosine + first * sine], axis=-1)

def reference(tokens, attn_gain, mlp_gain, w_query, w_key, value_projection, w_out, w_gate, w_up, w_down, lengths, page_table):
    token_index = jnp.arange(PACK_TOKENS, dtype=jnp.int32)
    segment, token_positions = segment_info(lengths, token_index)
    normed = rms_scale(tokens, attn_gain).astype(jnp.bfloat16)
    query = jnp.dot(normed, w_query, preferred_element_type=jnp.float32)
    unrotated_key = jnp.dot(normed, w_key, preferred_element_type=jnp.float32)
    value_raw = jnp.dot(normed, value_projection, preferred_element_type=jnp.float32)
    query_rot = apply_rotary(query.reshape(PACK_TOKENS, QUERY_HEAD_COUNT, HEAD_WIDTH), token_positions).astype(jnp.bfloat16)
    rotated_key = apply_rotary(unrotated_key.reshape(PACK_TOKENS, KEY_VALUE_HEADS, HEAD_WIDTH), token_positions).astype(jnp.bfloat16)
    value_vectors = value_raw.astype(jnp.bfloat16)
    group_width = QUERY_HEAD_COUNT // KEY_VALUE_HEADS
    query_heads = query_rot.transpose(1, 0, 2)
    key_heads = jnp.repeat(rotated_key.transpose(1, 0, 2), group_width, axis=0)
    per_head_values = jnp.repeat(value_vectors.reshape(PACK_TOKENS, KEY_VALUE_HEADS, HEAD_WIDTH).transpose(1, 0, 2), group_width, axis=0)
    distance = token_index[:, None] - token_index[None, :]
    allowed = (segment[:, None] == segment[None, :]) & (distance >= 0) & (distance < WIN)

    def one_head(operands):
        queries, keys, values = operands
        scores = jnp.einsum('qd,kd->qk', queries.astype(jnp.float32), keys.astype(jnp.float32)) * HEAD_WIDTH ** (-0.5)
        masked = jnp.where(allowed, scores, masked_score)
        top = lax.optimization_barrier(jnp.max(masked, axis=-1, keepdims=True))
        weights = jnp.where(allowed, jnp.exp(masked - top), 0.0)
        rounded = weights.astype(jnp.bfloat16)
        mixed = jnp.einsum('qk,kd->qd', rounded.astype(jnp.float32), values.astype(jnp.float32))
        return mixed / lax.optimization_barrier(jnp.sum(weights, axis=-1, keepdims=True))
    heads_out = lax.map(one_head, (query_heads, key_heads, per_head_values))
    attended = heads_out.transpose(1, 0, 2).reshape(PACK_TOKENS, QUERY_HEAD_COUNT * HEAD_WIDTH).astype(jnp.bfloat16)
    residual = (tokens.astype(jnp.float32) + jnp.dot(attended, w_out, preferred_element_type=jnp.float32)).astype(jnp.bfloat16)
    normed_mlp = rms_scale(residual, mlp_gain).astype(jnp.bfloat16)
    gate = jnp.dot(normed_mlp, w_gate, preferred_element_type=jnp.float32)
    up_values = jnp.dot(normed_mlp, w_up, preferred_element_type=jnp.float32)
    hidden = (jax.nn.silu(gate) * up_values).astype(jnp.bfloat16)
    layer_out = (residual.astype(jnp.float32) + jnp.dot(hidden, w_down, preferred_element_type=jnp.float32)).astype(jnp.bfloat16)
    flat_keys = rotated_key.reshape(PACK_TOKENS, KEY_VALUE_HEADS * HEAD_WIDTH)
    stacked_pairs = jnp.stack([flat_keys, value_vectors], axis=0).reshape(2, PACK_PAGES, PAGE_TOKENS, KEY_VALUE_HEADS * HEAD_WIDTH).transpose(1, 0, 2, 3)
    cache_cells = page_table[:, 0] * CACHE_GROUP_CELLS + page_table[:, 1]
    paged_key_value_cache = jnp.zeros((N_GX * CACHE_GROUP_CELLS, 2, PAGE_TOKENS, KEY_VALUE_HEADS * HEAD_WIDTH), jnp.bfloat16).at[cache_cells].set(stacked_pairs)
    return (layer_out, paged_key_value_cache)
```

```python
import functools

import jax
import jax.numpy as jnp
from jax import lax
from jax.experimental import pallas as pl
from jax.experimental.pallas import tpu as pltpu
from jax.sharding import PartitionSpec as P

HEAD = 128
PAGE = 32
WIDTH = 4096
GROUP = 512
LOCAL = 32
HIDDEN = 896
HALF = WIDTH // 2
QUARTER = WIDTH // 4
ROPE_BASE = 10000.0
EPS = 1e-05
MASKED = -1e30
F32 = jnp.float32
BF16 = jnp.bfloat16
MESH = pl.DeviceIdType.MESH
VMEM_LIMIT = 66_000_000


def mod4(value):
    return lax.rem(value + 4, 4)


def dot(a, b):
    return jnp.dot(a, b, preferred_element_type=F32)


class Net:
    def __init__(self, send, recv):
        self.send, self.recv, self.used, self.started = send, recv, 0, []
        self.g, self.h = lax.axis_index("gx"), lax.axis_index("gy")
        self.z, self.c = lax.div(self.g, 2), lax.rem(self.g, 2)
        self.x, self.y = lax.div(self.h, 4), lax.rem(self.h, 4)

    def along_z(self, d):
        return (mod4(self.z + d) * 2 + self.c, self.h)

    def partner(self):
        return (self.z * 2 + 1 - self.c, self.h)

    def plane(self, dx, dy):
        return (self.g, mod4(self.x + dx) * 4 + mod4(self.y + dy))

    def barrier(self):
        peers = [self.along_z(1), self.along_z(-1), self.partner()]
        peers += [self.plane(1, 0), self.plane(-1, 0), self.plane(0, 1), self.plane(0, -1)]
        sem = pltpu.get_barrier_semaphore()
        for peer in peers:
            pl.semaphore_signal(sem, inc=1, device_id=peer, device_id_type=MESH)
        pl.semaphore_wait(sem, len(peers))

    def put(self, src, dst, to):
        index = self.used
        self.used += 1
        copy = pltpu.make_async_remote_copy(
            src_ref=src,
            dst_ref=dst,
            send_sem=self.send.at[index],
            recv_sem=self.recv.at[index],
            device_id=to,
            device_id_type=MESH,
        )
        copy.start()
        self.started.append(copy)
        return (index, to)

    def got(self, tag, dst):
        index, to = tag
        pltpu.make_async_remote_copy(
            src_ref=dst,
            dst_ref=dst,
            send_sem=self.send.at[index],
            recv_sem=self.recv.at[index],
            device_id=to,
            device_id_type=MESH,
        ).wait_recv()

    def finish(self):
        for copy in self.started:
            copy.wait_send()
        self.started = []


class PlaneGather:
    def __init__(self, net, buf):
        self.net, self.buf = net, buf
        self.first, self.relay1, self.second, self.relay2 = {}, {}, {}, {}

    def view(self, h, da, db, q=None):
        n = self.net
        a, b = (n.x, n.y) if h == 0 else (n.y, n.x)
        a, b = mod4(a + da), mod4(b + db)
        slot = a * 4 + b if h == 0 else b * 4 + a
        cols = pl.ds(h * HALF, HALF) if q is None else pl.ds(h * HALF + q * QUARTER, QUARTER)
        return self.buf.at[slot, :, cols]

    def to(self, h, da, db):
        return self.net.plane(da, db) if h == 0 else self.net.plane(db, da)

    def put(self, h, da, db, q, ta, tb):
        ref = self.view(h, da, db, q)
        return self.net.put(ref, ref, self.to(h, ta, tb))

    def start(self):
        for h in (0, 1):
            for d in (1, -1):
                self.first[h, d] = self.put(h, 0, 0, None, d, 0)
        for h in (0, 1):
            for d in (1, -1):
                self.second[h, 0, d] = self.put(h, 0, 0, None, 0, d)

    def step1(self):
        for d in (1, -1):
            for h in (0, 1):
                self.net.got(self.first[h, d], self.view(h, -d, 0))
                self.relay1[h, d] = self.put(h, -d, 0, 0 if d == 1 else 1, d, 0)
                for e in (1, -1):
                    self.second[h, -d, e] = self.put(h, -d, 0, None, 0, e)

    def pass_on(self, j):
        for d in (1, -1):
            for h in (0, 1):
                self.net.got(self.second[h, j, d], self.view(h, j, -d))
                self.relay2[h, j, d] = self.put(h, j, -d, 0 if d == 1 else 1, 0, d)

    def step2(self):
        self.pass_on(0)

    def step3(self):
        for h in (0, 1):
            for d in (1, -1):
                self.net.got(self.relay1[h, d], self.view(h, 2, 0, 0 if d == 1 else 1))
            for e in (1, -1):
                self.second[h, 2, e] = self.put(h, 2, 0, None, 0, e)

    def step4(self):
        self.pass_on(-1)
        self.pass_on(1)

    def step5(self):
        self.pass_on(2)

    def step6(self):
        for j in (0, -1, 1, 2):
            for h in (0, 1):
                for d in (1, -1):
                    self.net.got(self.relay2[h, j, d], self.view(h, j, 2, 0 if d == 1 else 1))


class PlaneScatter:
    def __init__(self, net, part, near, far, total, small):
        self.net, self.part, self.total = net, part, total
        self.r1, self.ri, self.r2 = near, far, None
        self.near, self.small = near, small
        self.tags = {}

    def pos(self, h):
        n = self.net
        return (n.x, n.y) if h == 0 else (n.y, n.x)

    def to(self, h, ta, tb):
        return self.net.plane(ta, tb) if h == 0 else self.net.plane(tb, ta)

    def chunk(self, h, q, da):
        at = mod4(self.pos(h)[0] + da)
        cols = pl.ds(h * HALF + q * QUARTER, QUARTER)
        if h == 0:
            return self.part.at[at, :, :, cols]
        return self.part.at[:, at, :, cols]

    def row(self, h, q, db):
        return self.total.at[h * 2 + q, mod4(self.pos(h)[1] + db)]

    def step1(self, h, q):
        d = 1 if q == 0 else -1
        k = h * 2 + q
        self.tags[k, 0] = self.net.put(self.chunk(h, q, 2), self.near.at[k, 0], self.to(h, d, 0))
        self.tags[k, 1] = self.net.put(self.chunk(h, q, -d), self.near.at[k, 1], self.to(h, -d, 0))

    def step2(self, h, q):
        d = 1 if q == 0 else -1
        k = h * 2 + q
        self.net.got(self.tags[k, 0], self.near.at[k, 0])
        mine = self.chunk(h, q, d)
        mine[...] = (mine[...].astype(F32) + self.near[k, 0].astype(F32)).astype(BF16)
        self.tags[k, 2] = self.net.put(mine, self.near.at[k, 2], self.to(h, d, 0))

    def step3(self, h, q):
        d = 1 if q == 0 else -1
        k = h * 2 + q
        self.net.got(self.tags[k, 1], self.near.at[k, 1])
        self.net.got(self.tags[k, 2], self.near.at[k, 2])
        mine = self.chunk(h, q, 0)
        self.total[k] = (
            mine[...].astype(F32) + self.near[k, 1].astype(F32) + self.near[k, 2].astype(F32)
        ).astype(BF16)
        self.tags[k, 3] = self.net.put(self.row(h, q, 2), self.small.at[k, 0], self.to(h, 0, d))
        self.tags[k, 4] = self.net.put(self.row(h, q, -d), self.small.at[k, 1], self.to(h, 0, -d))

    def step4(self, h, q):
        d = 1 if q == 0 else -1
        k = h * 2 + q
        self.net.got(self.tags[k, 3], self.small.at[k, 0])
        mine = self.row(h, q, d)
        mine[...] = (mine[...].astype(F32) + self.small[k, 0].astype(F32)).astype(BF16)
        self.tags[k, 5] = self.net.put(mine, self.small.at[k, 2], self.to(h, 0, d))

    def step5(self, h, q):
        k = h * 2 + q
        self.net.got(self.tags[k, 4], self.small.at[k, 1])
        self.net.got(self.tags[k, 5], self.small.at[k, 2])
        mine = self.row(h, q, 0)
        return mine[...].astype(F32) + self.small[k, 1].astype(F32) + self.small[k, 2].astype(F32)


QUARTERS = ((0, 0), (1, 0), (0, 1), (1, 1))


class ColumnGather:
    def __init__(self, net, src, slot, sem, rows):
        self.net, self.src, self.slot, self.sem, self.rows = net, src, slot, sem, rows
        self.zs, self.relays, self.fwd, self.fwdr = {}, {}, {}, {}

    def at(self, dz, other=False, half=None):
        n = self.net
        core = 1 - n.c if other else n.c
        return self.slot(mod4(n.z + dz) * 2 + core, half)

    def start(self):
        n = self.net
        for d in (1, -1):
            self.zs[d] = n.put(self.src, self.at(0), n.along_z(d))

    def start_local(self):
        self.pair = self.net.put(self.src, self.at(0), self.net.partner())
        self.own = pltpu.make_async_copy(self.src, self.at(0), self.sem)
        self.own.start()

    def relay(self):
        n = self.net
        for d in (1, -1):
            n.got(self.zs[d], self.at(-d))
            part = self.at(-d, half=0 if d == 1 else 1)
            self.relays[d] = n.put(part, part, n.along_z(d))
            self.fwd[d] = n.put(self.at(-d), self.at(-d), n.partner())

    def forward(self):
        n = self.net
        for d in (1, -1):
            part = self.at(2, half=0 if d == 1 else 1)
            n.got(self.relays[d], part)
            self.fwdr[d] = n.put(part, part, n.partner())

    def wait(self):
        n = self.net
        self.own.wait()
        n.got(self.pair, self.at(0, True))
        for d in (1, -1):
            n.got(self.fwd[d], self.at(-d, True))
        for d in (1, -1):
            n.got(self.fwdr[d], self.at(2, True, 0 if d == 1 else 1))


def half_rows(buf, rows):
    def slot(index, half):
        if half is None:
            return buf.at[index]
        return buf.at[index, pl.ds(half * (rows // 2), rows // 2)]

    return slot


def rms(values, gain):
    mean_square = jnp.mean(values * values, axis=-1, keepdims=True)
    return values * lax.rsqrt(mean_square + EPS) * gain


def front_kernel(
    tokens, gain, cos, sin, wqkv, q_out, kv_out,
    x_all, w_all, pair_src, pair_all, send, recv, own_sem,
):
    net = Net(send, recv)
    net.barrier()
    weights = ColumnGather(net, wqkv, half_rows(w_all, GROUP), own_sem.at[0], GROUP)
    weights.start()
    lower = lax.rem(net.y, 2) == 0
    other = (net.g, net.x * 4 + net.y + 1 - 2 * lax.rem(net.y, 2))
    swap = net.put(wqkv.at[:, pl.ds(2 * HEAD, HEAD)], pair_src, other)
    weights.start_local()
    values = tokens[...].astype(F32)
    x_all[net.h] = rms(values, gain[...].astype(F32)).astype(BF16)
    gather = PlaneGather(net, x_all)
    gather.start()
    pairs = ColumnGather(net, pair_src, half_rows(pair_all, GROUP), own_sem.at[1], GROUP)
    net.got(swap, pair_src)
    pairs.start()
    pairs.start_local()
    gather.step1()
    gather.step2()
    weights.relay()
    gather.step3()
    pairs.relay()
    gather.step4()
    weights.forward()
    pairs.forward()
    gather.step5()
    weights.wait()
    pairs.wait()
    gather.step6()

    lane = lax.broadcasted_iota(jnp.int32, (256, HEAD), 1)
    low = lane < HEAD // 2

    @pl.loop(0, 2)
    def _(r):
        main = jnp.zeros((256, 3 * HEAD), F32)
        side = jnp.zeros((256, HEAD), F32)
        for k in range(8):
            rows = x_all[pl.ds(r * 8, 8), :, k * GROUP:(k + 1) * GROUP].reshape(256, GROUP)
            main = main + dot(rows, w_all[k])
            side = side + dot(rows, pair_all[k])
        c = cos[pl.ds(r * 256, 256), :]
        s = sin[pl.ds(r * 256, 256), :]

        def rotate(v):
            return (v * c + pltpu.roll(v, HEAD // 2, 1) * s).astype(BF16)

        mine = main[:, 2 * HEAD:]
        even = jnp.where(lower, mine, side)
        odd = jnp.where(lower, side, mine)
        key = jnp.where(low, even, pltpu.roll(odd, HEAD // 2, 1))
        value = jnp.where(low, pltpu.roll(even, HEAD // 2, 1), odd)
        at = pl.ds(r * 256, 256)
        q_out[at, 0:HEAD] = rotate(main[:, 0:HEAD])
        q_out[at, HEAD:2 * HEAD] = rotate(main[:, HEAD:2 * HEAD])
        kv_out[pl.ds(r * 8, 8), :, 0:HEAD] = rotate(key).reshape(8, PAGE, HEAD)
        kv_out[pl.ds(r * 8, 8), :, HEAD:2 * HEAD] = value.astype(BF16).reshape(8, PAGE, HEAD)

    net.finish()


def vmem():
    return pl.BlockSpec(memory_space=pltpu.VMEM)


def anywhere():
    return pl.BlockSpec(memory_space=pl.ANY)


def front(tokens, gain, cos, sin, wqkv):
    return pl.pallas_call(
        front_kernel,
        out_shape=(
            jax.ShapeDtypeStruct((GROUP, 2 * HEAD), BF16),
            jax.ShapeDtypeStruct((16, PAGE, 2 * HEAD), BF16),
        ),
        in_specs=[vmem()] * 4 + [anywhere()],
        out_specs=(vmem(), vmem()),
        scratch_shapes=[
            pltpu.VMEM((16, LOCAL, WIDTH), BF16),
            pltpu.VMEM((8, GROUP, 3 * HEAD), BF16),
            pltpu.VMEM((GROUP, HEAD), BF16),
            pltpu.VMEM((8, GROUP, HEAD), BF16),
            pltpu.SemaphoreType.DMA((64,)),
            pltpu.SemaphoreType.DMA((64,)),
            pltpu.SemaphoreType.DMA((2,)),
        ],
        compiler_params=pltpu.CompilerParams(
            collective_id=0, has_side_effects=True, vmem_limit_bytes=VMEM_LIMIT
        ),
        name="front",
    )(tokens, gain, cos, sin, wqkv)


def back_kernel(
    inv, q, kv, begin, tokens, gain, wo, wg, wu, wd, out, cache,
    kv_all, wo_all, wg_all, wu_all, wd_all, x_all, part, near, total, small,
    near2, total2, small2, hidden, resid, send, recv, own_sem,
):
    net = Net(send, recv)
    net.barrier()

    def kv_slot(index, half):
        if half is None:
            return kv_all.at[pl.ds(index * 16, 16)]
        return kv_all.at[pl.ds(index * 16 + half * 8, 8)]

    keys = ColumnGather(net, kv, kv_slot, own_sem.at[0], 16)
    outw = ColumnGather(net, wo, half_rows(wo_all, 256), own_sem.at[1], 256)
    gate = ColumnGather(net, wg, half_rows(wg_all, GROUP), own_sem.at[2], GROUP)
    up = ColumnGather(net, wu, half_rows(wu_all, GROUP), own_sem.at[3], GROUP)
    down = ColumnGather(net, wd, half_rows(wd_all, HIDDEN), own_sem.at[4], HIDDEN)
    keys.start()
    keys.start_local()
    outw.start()
    outw.start_local()
    keys.relay()
    outw.relay()
    gate.start()
    up.start()
    gate.start_local()
    up.start_local()
    down.start_local()
    keys.forward()
    keys.wait()

    first_key = net.g * GROUP
    query_index = first_key + lax.broadcasted_iota(jnp.int32, (GROUP, GROUP), 0)
    lane = lax.broadcasted_iota(jnp.int32, (GROUP, GROUP), 1)
    query_begin = begin[...]
    scale = HEAD ** (-0.5)
    for head in range(2):
        query = q[:, head * HEAD:(head + 1) * HEAD]

        def body(group, state):
            top, weight, mixed = state
            at = pl.ds(group * 16, 16)
            key = kv_all[at, :, 0:HEAD].reshape(GROUP, HEAD)
            value = kv_all[at, :, HEAD:2 * HEAD].reshape(GROUP, HEAD)
            scores = lax.dot_general(
                query, key, (((1,), (1,)), ((), ())), preferred_element_type=F32
            ) * scale
            index = lane + group * GROUP
            allowed = (index >= query_begin) & (index <= query_index)
            scores = jnp.where(allowed, scores, MASKED)
            newest = jnp.maximum(top, jnp.max(scores, axis=1, keepdims=True))
            weights = jnp.where(allowed, jnp.exp(scores - newest), 0.0)
            shrink = jnp.exp(top - newest)
            return (
                newest,
                weight * shrink + jnp.sum(weights, axis=1, keepdims=True),
                mixed * shrink + dot(weights.astype(BF16), value),
            )

        state = (
            jnp.full((GROUP, 1), MASKED, F32),
            jnp.zeros((GROUP, 1), F32),
            jnp.zeros((GROUP, HEAD), F32),
        )
        top, weight, mixed = lax.fori_loop(0, net.g + 1, body, state)
        hidden[:, head * HEAD:(head + 1) * HEAD] = (mixed / weight).astype(BF16)

    outw.forward()
    outw.wait()
    scatter = PlaneScatter(net, part, near, None, total, small)
    attended = hidden[:, 0:2 * HEAD]
    for h, q_at in QUARTERS:
        for e in range(2):
            k = (h * 2 + q_at) * 2 + e
            part[:, :, :, k * GROUP:(k + 1) * GROUP] = (
                dot(attended, wo_all[k]).astype(BF16).reshape(4, 4, LOCAL, GROUP)
            )
        scatter.step1(h, q_at)
    low = lax.rem(net.y, 2) == 0
    for s in range(16):
        page = kv_all[inv[s]].astype(F32)
        for e in range(2):
            both = page[:, e * HEAD:(e + 1) * HEAD]
            mine = jnp.where(low, both, pltpu.roll(both, HEAD // 2, 1))
            cache[s, e] = mine[:, 0:HEAD // 2].astype(BF16)
    for h, q_at in QUARTERS:
        scatter.step2(h, q_at)
    gate.relay()
    for h, q_at in QUARTERS:
        scatter.step3(h, q_at)
    for h, q_at in QUARTERS:
        scatter.step4(h, q_at)
    for h, q_at in QUARTERS:
        at = pl.ds((h * 2 + q_at) * QUARTER, QUARTER)
        share = scatter.step5(h, q_at)
        resid[:, at] = (tokens[:, at].astype(F32) + share).astype(BF16)
    x_all[net.h] = rms(resid[...].astype(F32), gain[...].astype(F32)).astype(BF16)
    gather = PlaneGather(net, x_all)
    gather.start()
    up.relay()
    down.start()
    gather.step1()
    gather.step2()
    gather.step3()
    gate.forward()
    gather.step4()
    gather.step5()
    gather.step6()
    gate.wait()
    up.forward()
    up.wait()

    @pl.loop(0, 2)
    def _(r):
        gates = jnp.zeros((256, HIDDEN), F32)
        ups = jnp.zeros((256, HIDDEN), F32)
        for k in range(8):
            rows = x_all[pl.ds(r * 8, 8), :, k * GROUP:(k + 1) * GROUP].reshape(256, GROUP)
            gates = gates + dot(rows, wg_all[k])
            ups = ups + dot(rows, wu_all[k])
        hidden[pl.ds(r * 256, 256), :] = (gates / (1.0 + jnp.exp(-gates)) * ups).astype(BF16)

    down.relay()
    down.forward()
    down.wait()
    net.finish()
    scatter = PlaneScatter(net, part, near2, None, total2, small2)
    for h, q_at in QUARTERS:
        for e in range(2):
            k = (h * 2 + q_at) * 2 + e
            part[:, :, :, k * GROUP:(k + 1) * GROUP] = (
                dot(hidden[...], wd_all[k]).astype(BF16).reshape(4, 4, LOCAL, GROUP)
            )
        scatter.step1(h, q_at)
    for h, q_at in QUARTERS:
        scatter.step2(h, q_at)
    for h, q_at in QUARTERS:
        scatter.step3(h, q_at)
    for h, q_at in QUARTERS:
        scatter.step4(h, q_at)
    for h, q_at in QUARTERS:
        at = pl.ds((h * 2 + q_at) * QUARTER, QUARTER)
        out[:, at] = (resid[:, at].astype(F32) + scatter.step5(h, q_at)).astype(BF16)
    net.finish()


def back(inv, q, kv, begin, tokens, gain, wo, wg, wu, wd):
    return pl.pallas_call(
        back_kernel,
        out_shape=(
            jax.ShapeDtypeStruct((LOCAL, WIDTH), BF16),
            jax.ShapeDtypeStruct((16, 2, PAGE, HEAD // 2), BF16),
        ),
        in_specs=[pl.BlockSpec(memory_space=pltpu.SMEM), vmem(), anywhere()]
        + [vmem()] * 3
        + [anywhere()] * 4,
        out_specs=(vmem(), vmem()),
        scratch_shapes=[
            pltpu.VMEM((128, PAGE, 2 * HEAD), BF16),
            pltpu.VMEM((8, 256, GROUP), BF16),
            pltpu.VMEM((8, GROUP, HIDDEN), BF16),
            pltpu.VMEM((8, GROUP, HIDDEN), BF16),
            pltpu.VMEM((8, HIDDEN, GROUP), BF16),
            pltpu.VMEM((16, LOCAL, WIDTH), BF16),
            pltpu.VMEM((4, 4, LOCAL, WIDTH), BF16),
            pltpu.VMEM((4, 3, 4, LOCAL, QUARTER), BF16),
            pltpu.VMEM((4, 4, LOCAL, QUARTER), BF16),
            pltpu.VMEM((4, 3, LOCAL, QUARTER), BF16),
            pltpu.VMEM((4, 3, 4, LOCAL, QUARTER), BF16),
            pltpu.VMEM((4, 4, LOCAL, QUARTER), BF16),
            pltpu.VMEM((4, 3, LOCAL, QUARTER), BF16),
            pltpu.VMEM((GROUP, HIDDEN), BF16),
            pltpu.VMEM((LOCAL, WIDTH), BF16),
            pltpu.SemaphoreType.DMA((160,)),
            pltpu.SemaphoreType.DMA((160,)),
            pltpu.SemaphoreType.DMA((5,)),
        ],
        compiler_params=pltpu.CompilerParams(
            collective_id=1, has_side_effects=True, vmem_limit_bytes=VMEM_LIMIT
        ),
        name="back",
    )(inv, q, kv, begin, tokens, gain, wo, wg, wu, wd)


def per_device(
    tokens, attn_gain, mlp_gain, w_query, w_key, value_projection,
    w_out, w_gate, w_up, w_down, lengths, page_table,
):
    group_index = lax.axis_index("gx")
    token_index = group_index * GROUP + jnp.arange(GROUP, dtype=jnp.int32)
    ends = jnp.sum(
        jnp.where(jnp.arange(6)[:, None] >= jnp.arange(6)[None, :], lengths[None, :], 0), axis=1
    )
    begin = jnp.max(jnp.where(token_index[:, None] >= ends[None, :], ends[None, :], 0), axis=1)
    position = (token_index - begin).astype(F32)
    lane = jnp.arange(HEAD, dtype=jnp.int32)
    freq = ROPE_BASE ** (-(lane % (HEAD // 2)).astype(F32) * 2.0 / HEAD)
    angle = position[:, None] * freq[None, :]
    cos = jnp.cos(angle)
    sin = jnp.sin(angle) * jnp.where(lane < HEAD // 2, -1.0, 1.0)[None, :]
    wqkv = jnp.concatenate([w_query, w_key, value_projection], axis=1)
    cells = page_table[:, 0] * 16 + page_table[:, 1]
    target = group_index * 16 + jnp.arange(16, dtype=jnp.int32)
    inv = jnp.sum(
        jnp.where(
            cells[None, :] == target[:, None], jnp.arange(128, dtype=jnp.int32)[None, :], 0
        ),
        axis=1,
    )
    q, kv = front(tokens, attn_gain[None, :], cos, sin, wqkv)
    return back(
        inv, q, kv, begin[:, None], tokens, mlp_gain[None, :], w_out, w_gate, w_up, w_down
    )


def solution(mesh):
    placed = (
        P(("gx", "gy"), None),
        P(),
        P(),
        P("gx", "gy"),
        P("gx", "gy"),
        P("gx", "gy"),
        P("gy", "gx"),
        P("gx", "gy"),
        P("gx", "gy"),
        P("gy", "gx"),
        P(),
        P(),
    )
    return jax.shard_map(
        per_device,
        mesh=mesh,
        in_specs=placed,
        out_specs=(P(("gx", "gy"), None), P("gx", None, None, "gy")),
        check_vma=False,
    )
```
